32 devices in a mesh: outer: 4 (over x, core), inner: 8 (over z, y).
Axes of the slice: x: 2, y: 2, z: 4, core: 2. Of those that a mesh axis runs over, the one named last changes fastest.
Arguments:
- query_rows: bfloat16 [12288, 2048], P(('outer', 'inner')), may hold values from -1.5 to 1.5
- key_rows: bfloat16 [12288, 2048], P(('outer', 'inner')), may hold values from -6 to 6
- value_rows: bfloat16 [12288, 2048], P(('outer', 'inner')), may hold values from -6 to 6
- grad_output: bfloat16 [12288, 2048], P(('outer', 'inner')), may hold values from -0.59765625 to 0.59765625
Outputs:
- grad_query: bfloat16 [12288, 2048], P(('outer', 'inner'))
- grad_key: bfloat16 [12288, 2048], P(('outer', 'inner'))
- grad_value: bfloat16 [12288, 2048], P(('outer', 'inner'))
The draws below stay inside these ranges and needn't reach their ends.
All inputs are finite; a program needn't handle non-finite values.
Results may differ from the reference program's by a relative error of at most 0.0058.
Values may be sent and summed in bfloat16 or wider, within the bound.
No kernel may reach another device: no remote copies, remote signals or barrier semaphores. Data moves between devices by JAX's collectives and lax.ppermute only.
A program may use at most 64 MiB of HBM per device.

```python
import jax
import jax.numpy as jnp
from jax import lax

HEADS = 16
HEAD = 128
TOK_DEV = 384
TOKENS = 12288


def block_levels(own_key, extent, pieces, smallest, largest):
    loudness = 1.0
    for dim, blocks in pieces:
        steps = jax.random.uniform(jax.random.fold_in(jax.random.fold_in(own_key, 6), dim), (blocks,), jnp.float32, smallest / len(pieces), largest / len(pieces))
        loudness = loudness * jnp.repeat(jnp.exp(steps), extent[dim] // blocks).reshape((-1,) + (1,) * (len(extent) - 1 - dim))
    return loudness


def normal_values(rng, shape, scale, most, cuts=(), kind=jnp.bfloat16):
    values = jax.random.normal(rng, shape, jnp.float32) * scale
    if len(cuts) > 0:
        values = block_levels(rng, shape, cuts, -0.22, 0.18) * values
    return jnp.clip(values, min=-most, max=most).astype(kind)


def setup_inputs(seed: int = 0) -> dict:
    streams_of = jax.random.split(jax.random.key(seed), 5)
    query_rows = normal_values(streams_of[0], (TOKENS, HEADS * HEAD), 0.25, 1.5, ((0, 32),))
    key_rows = normal_values(streams_of[1], (TOKENS, HEADS * HEAD), 1.0, 6.0, ((0, 32),))
    value_rows = normal_values(streams_of[2], (TOKENS, HEADS * HEAD), 1.0, 6.0, ((0, 32),))
    grad_output = normal_values(streams_of[3], (TOKENS, HEADS * HEAD), 0.1, 0.59765625, ((0, 32),))
    return {"query_rows": query_rows, "key_rows": key_rows, "value_rows": value_rows, "grad_output": grad_output}


def block_grads(query, key, value, grad, scales, prefix, suffix):
    query = query.astype(jnp.float32)
    key = key.astype(jnp.float32)
    value = value.astype(jnp.float32)
    grad = grad.astype(jnp.float32)
    order = lax.iota(jnp.int32, query.shape[0])
    causal = (order[None, :] <= order[:, None])[None]
    prod_out = jnp.einsum('the,she->hts', grad, value)
    prod_in = jnp.einsum('thd,shd->hts', query, key)
    weight_out = (jnp.where(causal, prod_out, 0.0) * scales[None, :, None]).astype(jnp.bfloat16).astype(jnp.float32)
    weight_in = (jnp.where(causal, prod_in, 0.0) * scales[None, :, None]).astype(jnp.bfloat16).astype(jnp.float32)
    prefix = prefix.astype(jnp.float32)
    suffix = suffix.astype(jnp.float32)
    grad_q = scales[:, None, None] * jnp.einsum('the,hde->thd', grad, prefix) + jnp.einsum('hts,shd->thd', weight_out, key)
    grad_k = jnp.einsum('she,hde->shd', value, suffix) + jnp.einsum('hts,thd->shd', weight_out, query)
    grad_v = jnp.einsum('shd,hde->she', key, suffix) + jnp.einsum('hts,the->she', weight_in, grad)
    return (grad_q.astype(jnp.bfloat16), grad_k.astype(jnp.bfloat16), grad_v.astype(jnp.bfloat16))

def reference(query_rows, key_rows, value_rows, grad_output):
    count = TOKENS // TOK_DEV

    def split(array):
        return array.reshape(count, TOK_DEV, HEADS, HEAD)
    positions = jnp.arange(TOKENS, dtype=jnp.float32).reshape(count, TOK_DEV)
    scales = 1.0 / jnp.sqrt(positions + 1.0)

    def forward(state, blocks):
        key, value = blocks
        update = jnp.einsum('shd,she->hde', key.astype(jnp.float32), value.astype(jnp.float32))
        return (state + update, state.astype(jnp.bfloat16))

    def backward(state, blocks):
        query, grad, block_scales = blocks
        scaled = (grad.astype(jnp.float32) * block_scales[:, None, None]).astype(jnp.bfloat16)
        update = jnp.einsum('thd,the->hde', query.astype(jnp.float32), scaled.astype(jnp.float32))
        return (state + update, state.astype(jnp.bfloat16))
    start = jnp.zeros((HEADS, HEAD, HEAD), jnp.float32)
    _, prefix_states = lax.scan(forward, start, (split(key_rows), split(value_rows)))
    _, suffix_states = lax.scan(backward, start, (split(query_rows), split(grad_output), scales), reverse=True)

    def one_block(blocks):
        return block_grads(*blocks)
    grad_q, grad_k, grad_v = lax.map(one_block, (split(query_rows), split(key_rows), split(value_rows), split(grad_output), scales, prefix_states, suffix_states))
    width = HEADS * HEAD
    return (grad_q.reshape(TOKENS, width), grad_k.reshape(TOKENS, width), grad_v.reshape(TOKENS, width))
```

```python
import functools

import jax
import jax.numpy as jnp
from jax import lax
from jax.experimental import pallas as pl
from jax.experimental.pallas import tpu as pltpu
from jax.sharding import PartitionSpec as P

HEAD = 128
TILE = 128
BF = jnp.bfloat16
F32 = jnp.float32


def dot(a, b, ca, cb):
    return lax.dot_general(a, b, (((ca,), (cb,)), ((), ())), preferred_element_type=F32)


def scale_of(offset, shape, dim):
    spots = (offset + lax.broadcasted_iota(jnp.int32, shape, dim)).astype(F32)
    return 1.0 / jnp.sqrt(spots + 1.0)


def columns(j):
    return slice(j * HEAD, (j + 1) * HEAD)


def state_kernel(scaled, parts, heads, info, left, right, *outs):
    spot = pl.program_id(0)
    for m in range(parts):

        @pl.when(spot == m)
        def _(m=m):
            b = right[...]
            if scaled:
                scales = scale_of(info[1], (b.shape[0], 1), 0)
                b = (b.astype(F32) * scales).astype(BF)
            for j in range(heads):
                part = dot(left[:, columns(j)], b[:, columns(j)], 0, 0)
                outs[m][columns(j), :] = part.astype(BF)


def states(info, left, right, parts, scaled):
    length, width = left.shape
    step = width // parts
    heads = step // HEAD
    spec = pl.BlockSpec((length, step), lambda m, s: (0, s[0] ^ m))
    whole = pl.BlockSpec((step, HEAD), lambda m, s: (0, 0))
    return pl.pallas_call(
        functools.partial(state_kernel, scaled, parts, heads),
        grid_spec=pltpu.PrefetchScalarGridSpec(
            num_scalar_prefetch=1,
            grid=(parts,),
            in_specs=[spec, spec],
            out_specs=[whole] * parts,
        ),
        out_shape=[jax.ShapeDtypeStruct((step, HEAD), BF)] * parts,
        cost_estimate=pl.CostEstimate(
            flops=2 * length * width * HEAD,
            bytes_accessed=4 * length * width + 2 * width * HEAD,
            transcendentals=0,
        ),
        name="states_suffix" if scaled else "states_prefix",
    )(info, left, right)


def local_kv_kernel(info, query, key, value, grad, out_k, out_v):
    length = query.shape[0]
    scales = scale_of(info[1], (1, length), 1)
    for s in range(length // TILE):
        rows = slice(s * TILE, (s + 1) * TILE)
        later = slice(s * TILE, length)
        shape = (TILE, length - s * TILE)
        keep = lax.broadcasted_iota(jnp.int32, shape, 0) <= lax.broadcasted_iota(jnp.int32, shape, 1)
        w_out = dot(value[rows, :], grad[later, :], 1, 1)
        w_in = dot(key[rows, :], query[later, :], 1, 1)
        w_out = (jnp.where(keep, w_out, 0.0) * scales[:, later]).astype(BF)
        w_in = (jnp.where(keep, w_in, 0.0) * scales[:, later]).astype(BF)
        out_k[rows, :] = dot(w_out, query[later, :], 1, 0).astype(BF)
        out_v[rows, :] = dot(w_in, grad[later, :], 1, 0).astype(BF)


def local_q_kernel(info, key, value, grad, out_q):
    length = key.shape[0]
    scales = scale_of(info[1], (length, 1), 0)
    for t in range(length // TILE):
        rows = slice(t * TILE, (t + 1) * TILE)
        earlier = slice(0, (t + 1) * TILE)
        shape = (TILE, (t + 1) * TILE)
        keep = lax.broadcasted_iota(jnp.int32, shape, 1) <= lax.broadcasted_iota(jnp.int32, shape, 0) + t * TILE
        w_out = dot(grad[rows, :], value[earlier, :], 1, 1)
        w_out = (jnp.where(keep, w_out, 0.0) * scales[rows, :]).astype(BF)
        out_q[rows, :] = dot(w_out, key[earlier, :], 1, 0).astype(BF)


def local_part(kernel, info, args, outs, name):
    length, width = args[0].shape
    spec = pl.BlockSpec((length, HEAD), lambda j, s: (0, j))
    return pl.pallas_call(
        kernel,
        grid_spec=pltpu.PrefetchScalarGridSpec(
            num_scalar_prefetch=1,
            grid=(width // HEAD,),
            in_specs=[spec] * len(args),
            out_specs=[spec] * outs,
        ),
        out_shape=[jax.ShapeDtypeStruct((length, width), BF)] * outs,
        cost_estimate=pl.CostEstimate(
            flops=4 * outs * length * length * width,
            bytes_accessed=2 * (len(args) + outs) * length * width,
            transcendentals=0,
        ),
        name=name,
    )(info, *args)


def final_kv_kernel(parts, heads, info, key, value, part_k, part_v, *rest):
    pieces, (out_k, out_v) = rest[:parts], rest[parts:]
    spot = pl.program_id(0)
    for m in range(parts):

        @pl.when(spot == m)
        def _(m=m):
            for j in range(heads):
                c = columns(j)
                state = pieces[m][c, :]
                grad_k = dot(value[:, c], state, 1, 1) + part_k[:, c].astype(F32)
                grad_v = dot(key[:, c], state, 1, 0) + part_v[:, c].astype(F32)
                out_k[:, c] = grad_k.astype(BF)
                out_v[:, c] = grad_v.astype(BF)


def final_q_kernel(parts, heads, info, grad, part_q, *rest):
    pieces, (out_q,) = rest[:parts], rest[parts:]
    spot = pl.program_id(0)
    scales = scale_of(info[1], (grad.shape[0], 1), 0)
    for m in range(parts):

        @pl.when(spot == m)
        def _(m=m):
            for j in range(heads):
                c = columns(j)
                grad_q = dot(grad[:, c], pieces[m][c, :], 1, 1) * scales
                out_q[:, c] = (grad_q + part_q[:, c].astype(F32)).astype(BF)


def final_part(kernel, info, args, pieces, outs, name):
    length, width = args[0].shape
    parts = len(pieces)
    step = width // parts
    spec = pl.BlockSpec((length, step), lambda m, s: (0, s[0] ^ m))
    whole = pl.BlockSpec((step, HEAD), lambda m, s: (0, 0))
    return pl.pallas_call(
        functools.partial(kernel, parts, step // HEAD),
        grid_spec=pltpu.PrefetchScalarGridSpec(
            num_scalar_prefetch=1,
            grid=(parts,),
            in_specs=[spec] * len(args) + [whole] * parts,
            out_specs=[spec] * outs,
        ),
        out_shape=[jax.ShapeDtypeStruct((length, width), BF)] * outs,
        cost_estimate=pl.CostEstimate(
            flops=2 * outs * length * HEAD * width,
            bytes_accessed=2 * (len(args) + outs) * length * width,
            transcendentals=0,
        ),
        name=name,
    )(info, *args, *pieces)


def total(terms):
    out = terms[0].astype(F32)
    for term in terms[1:]:
        out = out + term.astype(F32)
    return out


def pick(condition, term):
    return jnp.where(condition, term.astype(F32), 0.0)


def entering(own, quad, reverse):
    count = lax.axis_size("inner")
    groups = lax.axis_size("outer")
    place = lax.axis_index("inner")
    q, h = place % quad, place // quad

    def precedes(a, b):
        return a > b if reverse else a < b

    def quad_swap(pieces):
        moved = [
            lax.ppermute(pieces[m], "inner", [(i, i ^ m) for i in range(count)])
            for m in range(1, quad)
        ]
        return [pieces[0]] + moved

    blocks = quad_swap(own)
    quad_sum = total(blocks).astype(BF)
    steps = range(1, groups)
    if reverse:
        hops = [[(i, i - k) for i in range(k, groups)] for k in steps]
    else:
        hops = [[(i, i + k) for i in range(groups - k)] for k in steps]
    outer = total([lax.ppermute(quad_sum, "outer", hop) for hop in hops])
    base = outer
    for k in range(1, count // quad):
        sent = (outer + pick(precedes(h, h ^ k), quad_sum)).astype(BF)
        swap = [(i, i ^ (k * quad)) for i in range(count)]
        base = base + lax.ppermute(sent, "inner", swap).astype(F32)
    out = []
    for m in range(quad):
        piece = base
        for n in range(quad):
            if n != m:
                piece = piece + pick(precedes(q ^ n, q ^ m), blocks[n])
        out.append(piece.astype(BF))
    return quad_swap(out)


def local(query, key, value, grad):
    length = query.shape[0]
    count = lax.axis_size("inner")
    quad = 1 << (count.bit_length() // 2)
    place = lax.axis_index("inner")
    block = lax.axis_index("outer") * count + place
    info = jnp.stack([place % quad, block * length]).astype(jnp.int32)
    own_suffix = states(info, query, grad, quad, True)
    own_prefix = states(info, key, value, quad, False)
    suffix = entering(own_suffix, quad, True)
    prefix = entering(own_prefix, quad, False)
    part_k, part_v = local_part(local_kv_kernel, info, (query, key, value, grad), 2, "local_kv")
    (part_q,) = local_part(local_q_kernel, info, (key, value, grad), 1, "local_q")
    grad_k, grad_v = final_part(final_kv_kernel, info, (key, value, part_k, part_v), suffix, 2, "final_kv")
    (grad_q,) = final_part(final_q_kernel, info, (grad, part_q), prefix, 1, "final_q")
    return grad_q, grad_k, grad_v


def solution(mesh):
    placed = P(("outer", "inner"), None)
    return jax.shard_map(
        local,
        mesh=mesh,
        in_specs=(placed,) * 4,
        out_specs=(placed,) * 3,
        check_vma=False,
    )
```

```python
import functools

import jax
import jax.numpy as jnp
from jax import lax
from jax.experimental import pallas as pl
from jax.experimental.pallas import tpu as pltpu
from jax.sharding import PartitionSpec as P

HEAD = 128
BF = jnp.bfloat16
F32 = jnp.float32
VMEM = pl.BlockSpec(memory_space=pltpu.VMEM)


def dot(a, b, ca, cb):
    return lax.dot_general(a, b, (((ca,), (cb,)), ((), ())), preferred_element_type=F32)


def places(length, parts):
    count = lax.axis_size("inner")
    place = lax.axis_index("inner")
    block = lax.axis_index("outer") * count + place
    return lax.rem(place, parts), block * length


def scale_of(offset, shape, dim):
    spots = (offset + lax.broadcasted_iota(jnp.int32, shape, dim)).astype(F32)
    return 1.0 / jnp.sqrt(spots + 1.0)


def lanes(start, j):
    return pl.ds(pl.multiple_of(start + j * HEAD, HEAD), HEAD)


def rows(j):
    return slice(j * HEAD, (j + 1) * HEAD)


def call(kernel, args, outs, flops, name):
    moved = sum(x.size * x.dtype.itemsize for x in (*args, *outs))
    return pl.pallas_call(
        kernel,
        in_specs=[VMEM] * len(args),
        out_specs=[VMEM] * len(outs),
        out_shape=outs,
        compiler_params=pltpu.CompilerParams(vmem_limit_bytes=16 << 20),
        cost_estimate=pl.CostEstimate(flops=flops, bytes_accessed=moved, transcendentals=0),
        name=name,
    )(*args)


def state_kernel(scaled, parts, left, right, *outs):
    length, width = left.shape
    step = width // parts
    q, offset = places(length, parts)
    scales = scale_of(offset, (length, 1), 0)
    for m in range(parts):
        for j in range(step // HEAD):
            c = lanes((q ^ m) * step, j)
            b = right[:, c]
            if scaled:
                b = (b.astype(F32) * scales).astype(BF)
            outs[m][rows(j), :] = dot(left[:, c], b, 0, 0).astype(BF)


def states(left, right, parts, scaled):
    length, width = left.shape
    return call(
        functools.partial(state_kernel, scaled, parts),
        (left, right),
        [jax.ShapeDtypeStruct((width // parts, HEAD), BF)] * parts,
        2 * length * width * HEAD,
        "states_suffix" if scaled else "states_prefix",
    )


def local_kernel(parts, m, query, key, value, grad, out_q, out_k, out_v):
    length, width = query.shape
    step = width // parts
    q, offset = places(length, parts)
    square = (length, length)
    down = lax.broadcasted_iota(jnp.int32, square, 0)
    across = lax.broadcasted_iota(jnp.int32, square, 1)
    by_row = jnp.where(across <= down, jnp.broadcast_to(scale_of(offset, (length, 1), 0), square), 0.0)
    by_column = jnp.where(down <= across, jnp.broadcast_to(scale_of(offset, (1, length), 1), square), 0.0)
    for j in range(step // HEAD):
        c = lanes((q ^ m) * step, j)
        o = rows(j)
        weights = (dot(grad[:, c], value[:, c], 1, 1) * by_row).astype(BF)
        out_q[:, o] = dot(weights, key[:, c], 1, 0).astype(BF)
        weights = (dot(value[:, c], grad[:, c], 1, 1) * by_column).astype(BF)
        out_k[:, o] = dot(weights, query[:, c], 1, 0).astype(BF)
        weights = (dot(key[:, c], query[:, c], 1, 1) * by_column).astype(BF)
        out_v[:, o] = dot(weights, grad[:, c], 1, 0).astype(BF)


def local_part(m, args, parts):
    length, width = args[0].shape
    step = width // parts
    return call(
        functools.partial(local_kernel, parts, m),
        args,
        [jax.ShapeDtypeStruct((length, step), BF)] * 3,
        12 * length * length * step,
        f"local_{m}",
    )


def final_kv_kernel(parts, key, value, *rest):
    pieces, part_k, part_v = rest[:parts], rest[parts : 2 * parts], rest[2 * parts : 3 * parts]
    out_k, out_v = rest[3 * parts :]
    length, width = key.shape
    step = width // parts
    q, _ = places(length, parts)
    for m in range(parts):
        for j in range(step // HEAD):
            c = lanes((q ^ m) * step, j)
            o = rows(j)
            state = pieces[m][o, :]
            out_k[:, c] = (dot(value[:, c], state, 1, 1) + part_k[m][:, o].astype(F32)).astype(BF)
            out_v[:, c] = (dot(key[:, c], state, 1, 0) + part_v[m][:, o].astype(F32)).astype(BF)


def final_q_kernel(parts, grad, *rest):
    pieces, part_q, out_q = rest[:parts], rest[parts : 2 * parts], rest[2 * parts]
    length, width = grad.shape
    step = width // parts
    q, offset = places(length, parts)
    scales = scale_of(offset, (length, 1), 0)
    for m in range(parts):
        for j in range(step // HEAD):
            c = lanes((q ^ m) * step, j)
            o = rows(j)
            grad_q = dot(grad[:, c], pieces[m][o, :], 1, 1) * scales
            out_q[:, c] = (grad_q + part_q[m][:, o].astype(F32)).astype(BF)


def final_part(kernel, args, pieces, parts, outs, name):
    length, width = args[0].shape
    return call(
        functools.partial(kernel, len(pieces)),
        (*args, *pieces, *parts),
        [jax.ShapeDtypeStruct((length, width), BF)] * outs,
        2 * outs * length * HEAD * width,
        name,
    )


def total(terms):
    out = terms[0].astype(F32)
    for term in terms[1:]:
        out = out + term.astype(F32)
    return out


def pick(condition, term):
    return jnp.where(condition, term.astype(F32), 0.0)


def entering(own, quad, reverse):
    count = lax.axis_size("inner")
    groups = lax.axis_size("outer")
    place = lax.axis_index("inner")
    q, h = place % quad, place // quad

    def precedes(a, b):
        return a > b if reverse else a < b

    def quad_swap(pieces):
        moved = [
            lax.ppermute(pieces[m], "inner", [(i, i ^ m) for i in range(count)])
            for m in range(1, quad)
        ]
        return [pieces[0]] + moved

    blocks = quad_swap(own)
    quad_sum = total(blocks).astype(BF)
    g = lax.axis_index("outer")
    outer = jnp.zeros(quad_sum.shape, F32)
    for k in range(1, groups):
        moved = lax.ppermute(quad_sum, "outer", [(i, i ^ k) for i in range(groups)])
        outer = outer + pick(precedes(g ^ k, g), moved)
    base = outer
    for k in range(1, count // quad):
        sent = (outer + pick(precedes(h, h ^ k), quad_sum)).astype(BF)
        swap = [(i, i ^ (k * quad)) for i in range(count)]
        base = base + lax.ppermute(sent, "inner", swap).astype(F32)
    out = []
    for m in range(quad):
        piece = base
        for n in range(quad):
            if n != m:
                piece = piece + pick(precedes(q ^ n, q ^ m), blocks[n])
        out.append(piece.astype(BF))
    return quad_swap(out)


def local(query, key, value, grad):
    count = lax.axis_size("inner")
    quad = 1 << (count.bit_length() // 2)
    own_suffix = states(query, grad, quad, True)
    own_prefix = states(key, value, quad, False)
    suffix = entering(own_suffix, quad, True)
    prefix = entering(own_prefix, quad, False)
    parts = [local_part(m, (query, key, value, grad), quad) for m in range(quad)]
    part_q, part_k, part_v = zip(*parts)
    grad_k, grad_v = final_part(final_kv_kernel, (key, value), suffix, part_k + part_v, 2, "final_kv")
    (grad_q,) = final_part(final_q_kernel, (grad,), prefix, part_q, 1, "final_q")
    return grad_q, grad_k, grad_v


def solution(mesh):
    placed = P(("outer", "inner"), None)
    return jax.shard_map(
        local,
        mesh=mesh,
        in_specs=(placed,) * 4,
        out_specs=(placed,) * 3,
        check_vma=False,
    )
```

```python
import functools

import jax
import jax.numpy as jnp
from jax import lax
from jax.experimental import pallas as pl
from jax.experimental.pallas import tpu as pltpu
from jax.sharding import PartitionSpec as P

HEAD = 128
BF = jnp.bfloat16
F32 = jnp.float32
VMEM = pl.BlockSpec(memory_space=pltpu.VMEM)


def dot(a, b, ca, cb):
    return lax.dot_general(a, b, (((ca,), (cb,)), ((), ())), preferred_element_type=F32)


def places(length, parts):
    count = lax.axis_size("inner")
    place = lax.axis_index("inner")
    block = lax.axis_index("outer") * count + place
    return lax.rem(place, parts), block * length


def scale_of(offset, shape, dim):
    spots = (offset + lax.broadcasted_iota(jnp.int32, shape, dim)).astype(F32)
    return 1.0 / jnp.sqrt(spots + 1.0)


def lanes(start, j):
    return pl.ds(pl.multiple_of(start + j * HEAD, HEAD), HEAD)


def rows(j):
    return slice(j * HEAD, (j + 1) * HEAD)


def call(kernel, args, outs, flops, name, space=VMEM, scratch=(), kept=True):
    moved = sum(x.size * x.dtype.itemsize for x in (*args, *outs))
    return pl.pallas_call(
        kernel,
        in_specs=[space] * len(args),
        out_specs=[VMEM] * len(outs),
        out_shape=[pltpu.VMEM(x.shape, x.dtype) for x in outs] if kept else outs,
        scratch_shapes=scratch,
        compiler_params=pltpu.CompilerParams(vmem_limit_bytes=16 << 20),
        cost_estimate=pl.CostEstimate(flops=flops, bytes_accessed=moved, transcendentals=0),
        name=name,
    )(*args)


def state_kernel(scaled, parts, left_hbm, right_hbm, left, right, *rest):
    outs, sems = rest[:parts], rest[parts]
    length, width = left.shape
    step = width // parts
    q, offset = places(length, parts)
    order = [*range(1, parts), 0]
    copies = []
    for m in order:
        spot = pl.ds(pl.multiple_of((q ^ m) * step, step), step)
        for n, (src, dst) in enumerate(((left_hbm, left), (right_hbm, right))):
            copy = pltpu.make_async_copy(src.at[:, spot], dst.at[:, spot], sems.at[m, n])
            copy.start()
            copies.append(copy)
    scales = scale_of(offset, (length, 1), 0)
    for i, m in enumerate(order):
        copies[2 * i].wait()
        copies[2 * i + 1].wait()
        for j in range(step // HEAD):
            c = lanes((q ^ m) * step, j)
            b = right[:, c]
            if scaled:
                b = (b.astype(F32) * scales).astype(BF)
            outs[m][rows(j), :] = dot(left[:, c], b, 0, 0).astype(BF)


def states(left, right, parts, scaled):
    length, width = left.shape
    return call(
        functools.partial(state_kernel, scaled, parts),
        [pltpu.with_memory_space_constraint(x, pltpu.MemorySpace.HBM) for x in (left, right)],
        [jax.ShapeDtypeStruct((length, width), BF)] * 2
        + [jax.ShapeDtypeStruct((width // parts, HEAD), BF)] * parts,
        2 * length * width * HEAD,
        "states_suffix" if scaled else "states_prefix",
        pl.BlockSpec(memory_space=pltpu.MemorySpace.HBM),
        [pltpu.SemaphoreType.DMA((parts, 2))],
    )


def local_kernel(parts, m, query, key, value, grad, out_q, out_k, out_v):
    length, width = query.shape
    step = width // parts
    q, offset = places(length, parts)
    square = (length, length)
    down = lax.broadcasted_iota(jnp.int32, square, 0)
    across = lax.broadcasted_iota(jnp.int32, square, 1)
    by_row = jnp.where(across <= down, jnp.broadcast_to(scale_of(offset, (length, 1), 0), square), 0.0)
    by_column = jnp.where(down <= across, jnp.broadcast_to(scale_of(offset, (1, length), 1), square), 0.0)
    for j in range(step // HEAD):
        c = lanes((q ^ m) * step, j)
        o = rows(j)
        weights = (dot(grad[:, c], value[:, c], 1, 1) * by_row).astype(BF)
        out_q[:, o] = dot(weights, key[:, c], 1, 0).astype(BF)
        weights = (dot(value[:, c], grad[:, c], 1, 1) * by_column).astype(BF)
        out_k[:, o] = dot(weights, query[:, c], 1, 0).astype(BF)
        weights = (dot(key[:, c], query[:, c], 1, 1) * by_column).astype(BF)
        out_v[:, o] = dot(weights, grad[:, c], 1, 0).astype(BF)


def local_part(m, args, parts):
    length, width = args[0].shape
    step = width // parts
    return call(
        functools.partial(local_kernel, parts, m),
        args,
        [jax.ShapeDtypeStruct((length, step), BF)] * 3,
        12 * length * length * step,
        f"local_{m}",
    )


def final_kv_kernel(parts, key, value, *rest):
    pieces, part_k, part_v = rest[:parts], rest[parts : 2 * parts], rest[2 * parts : 3 * parts]
    out_k, out_v = rest[3 * parts :]
    length, width = key.shape
    step = width // parts
    q, _ = places(length, parts)
    for m in range(parts):
        for j in range(step // HEAD):
            c = lanes((q ^ m) * step, j)
            o = rows(j)
            state = pieces[m][o, :]
            out_k[:, c] = (dot(value[:, c], state, 1, 1) + part_k[m][:, o].astype(F32)).astype(BF)
            out_v[:, c] = (dot(key[:, c], state, 1, 0) + part_v[m][:, o].astype(F32)).astype(BF)


def final_q_kernel(parts, grad, *rest):
    pieces, part_q, out_q = rest[:parts], rest[parts : 2 * parts], rest[2 * parts]
    length, width = grad.shape
    step = width // parts
    q, offset = places(length, parts)
    scales = scale_of(offset, (length, 1), 0)
    for m in range(parts):
        for j in range(step // HEAD):
            c = lanes((q ^ m) * step, j)
            o = rows(j)
            grad_q = dot(grad[:, c], pieces[m][o, :], 1, 1) * scales
            out_q[:, c] = (grad_q + part_q[m][:, o].astype(F32)).astype(BF)


def final_part(kernel, args, pieces, parts, outs, name):
    length, width = args[0].shape
    return call(
        functools.partial(kernel, len(pieces)),
        (*args, *pieces, *parts),
        [jax.ShapeDtypeStruct((length, width), BF)] * outs,
        2 * outs * length * HEAD * width,
        name,
        kept=False,
    )


def spread_kernel(parts, reverse, outer, *rest):
    others, blocks, outs = rest[: -2 * parts], rest[-2 * parts : -parts], rest[-parts:]
    q = lax.rem(lax.axis_index("inner"), parts)
    base = outer[...]
    for other in others:
        base = base + other[...].astype(F32)
    terms = [block[...].astype(F32) for block in blocks]
    for m in range(parts):
        piece = base
        for n in range(parts):
            if n != m:
                ahead = (q ^ n) > (q ^ m) if reverse else (q ^ n) < (q ^ m)
                piece = piece + jnp.where(ahead, terms[n], 0.0)
        outs[m][...] = piece.astype(BF)


def total(terms):
    out = terms[0].astype(F32)
    for term in terms[1:]:
        out = out + term.astype(F32)
    return out


def pick(condition, term):
    return jnp.where(condition, term.astype(F32), 0.0)


def entering(own, quad, reverse):
    count = lax.axis_size("inner")
    groups = lax.axis_size("outer")
    place = lax.axis_index("inner")
    q, h = place % quad, place // quad

    def precedes(a, b):
        return a > b if reverse else a < b

    def quad_swap(pieces):
        moved = [
            lax.ppermute(pieces[m], "inner", [(i, i ^ m) for i in range(count)])
            for m in range(1, quad)
        ]
        return [pieces[0]] + moved

    blocks = quad_swap(own)
    quad_sum = total(blocks).astype(BF)
    g = lax.axis_index("outer")
    outer = jnp.zeros(quad_sum.shape, F32)
    reach = quad_sum
    k = 1
    while k < groups:
        moved = lax.ppermute(reach, "outer", [(i, i ^ k) for i in range(groups)])
        outer = outer + pick(precedes(g ^ k, g), moved)
        reach = total([reach, moved]).astype(BF)
        k *= 2
    others = []
    for k in range(1, count // quad):
        sent = (outer + pick(precedes(h, h ^ k), quad_sum)).astype(BF)
        others.append(lax.ppermute(sent, "inner", [(i, i ^ (k * quad)) for i in range(count)]))
    pieces = call(
        functools.partial(spread_kernel, quad, reverse),
        (outer, *others, *blocks),
        [jax.ShapeDtypeStruct(quad_sum.shape, BF)] * quad,
        quad * quad * quad_sum.size,
        "spread_suffix" if reverse else "spread_prefix",
    )
    return quad_swap(pieces)


def local(query, key, value, grad):
    count = lax.axis_size("inner")
    quad = 1 << (count.bit_length() // 2)
    query, grad, *own_suffix = states(query, grad, quad, True)
    key, value, *own_prefix = states(key, value, quad, False)
    suffix = entering(own_suffix, quad, True)
    prefix = entering(own_prefix, quad, False)
    parts = [local_part(m, (query, key, value, grad), quad) for m in range(quad)]
    part_q, part_k, part_v = zip(*parts)
    grad_k, grad_v = final_part(final_kv_kernel, (key, value), suffix, part_k + part_v, 2, "final_kv")
    grad, grad_k, grad_v = lax.optimization_barrier((grad, grad_k, grad_v))
    (grad_q,) = final_part(final_q_kernel, (grad,), prefix, part_q, 1, "final_q")
    return grad_q, grad_k, grad_v


def solution(mesh):
    placed = P(("outer", "inner"), None)
    return jax.shard_map(
        local,
        mesh=mesh,
        in_specs=(placed,) * 4,
        out_specs=(placed,) * 3,
        check_vma=False,
    )
```
